128 devices in a mesh: branch: 8 (over x_hi, y), dp: 16 (over z, x_lo, core).
Axes of the slice: x: 4 (x_hi: 2, x_lo: 2; x = x_hi * 2 + x_lo), y: 4, z: 4, core: 2. Of those that a mesh axis runs over, the one named last changes fastest.
Arguments:
- hidden_in: bfloat16 [2048, 4096], P('dp', 'branch'), may hold values from -6 to 6
- context: bfloat16 [2048, 4096], P('dp'), may hold values from -6 to 6
- branch_wo: bfloat16 [8, 4096, 4096], P('branch', 'dp'), may hold values from -0.09375 to 0.09375
- expert_ids: int32 [2048, 2], P('dp'), may hold values from 0 to 7, all different within a row; in each aligned block of 128 rows (0 to 127, 128 to 255, ...) at most 48 rows name the same one
- gate_num: int32 [2048, 2], P('dp'), may hold values from 1 to 16
- w_gate: bfloat16 [8, 4096, 7168], P('branch', None, 'dp'), may hold values from -0.09375 to 0.09375
- w_up: bfloat16 [8, 4096, 7168], P('branch', None, 'dp'), may hold values from -0.09375 to 0.09375
- w_down: bfloat16 [8, 7168, 4096], P('branch', 'dp'), may hold values from -0.0625 to 0.0625
- cotangent: bfloat16 [2048, 4096], P('dp', 'branch'), may hold values from -6 to 6
Outputs:
- mixed: bfloat16 [2048, 4096], P('dp', 'branch')
- input_grad: bfloat16 [2048, 4096], P('dp', 'branch')
- grad_gate: bfloat16 [8, 4096, 7168], P('branch', None, 'dp')
- grad_up: bfloat16 [8, 4096, 7168], P('branch', None, 'dp')
- grad_down: bfloat16 [8, 7168, 4096], P('branch', 'dp')
The draws below stay inside these ranges and needn't reach their ends.
Inputs may be any that keep to these rules, and one draw needn't show every extreme that they name: `expert_ids`: the two ids of a row differ. In each aligned block of 128 rows no expert is named by more than 48 rows, and in some block one expert is named by exactly 48 rows.
All inputs are finite; a program needn't handle non-finite values.
Results may differ from the reference program's by a relative error of at most 0.019.
Values may be sent and summed in bfloat16 or wider, within the bound.
A program may use at most 128 MiB of HBM per device.

```python
import math
import jax
import jax.numpy as jnp
import numpy as np
from jax import lax

D = 4096
FF = 7168
TOK_DEV = 128
EXPERTS = 8
CAP = 48
TOKENS = 2048
N_DP = 16


def plant(array, own_key, smallest, top_value):
    longest = array.shape.index(max(array.shape))
    spots = []
    for shift in (0, 1):
        where = [jax.random.randint(jax.random.fold_in(own_key, axis), (), 0, length) for axis, length in enumerate(array.shape)]
        where[longest] = (where[longest] + shift) % array.shape[longest]
        spots.append(tuple(where))
    return array.at[spots[0]].set(smallest).at[spots[1]].set(top_value)


def steps_of(rng, extent, shards, least, high):
    loudness = 1.0
    for axis_at, blocks in shards:
        heights = jax.random.uniform(jax.random.fold_in(jax.random.fold_in(rng, 6), axis_at), (blocks,), jnp.float32, least / len(shards), high / len(shards))
        loudness = loudness * jnp.repeat(jnp.exp(heights), extent[axis_at] // blocks).reshape((-1,) + (1,) * (len(extent) - 1 - axis_at))
    return loudness


def shared_out(key, own, number, rows, count, top, most, slope):
    order = jax.random.permutation(key, count)
    packed, common = shares(count, rows * top, most, slope, True), shares(count, rows * top, most, slope, False)
    places = jnp.arange(count)

    def named(lengths, rotation):
        used = int((lengths > 0).sum())
        fixed = max(1, used // 4)
        passed = fixed + (places - fixed + rotation * (used - fixed)) % max(1, count - fixed)
        return jnp.zeros((count,), jnp.int32).at[order[jnp.where(places < fixed, places, passed)]].set(jnp.asarray(lengths, jnp.int32))

    lengths = jnp.where(number % 4 == 0, named(packed, number // 4), named(common, number - number // 4 - 1))
    mixed = jax.random.permutation(jax.random.fold_in(own, 3), count)
    donor, sink = mixed[0:count // 2 * 2:2], mixed[1:count // 2 * 2:2]
    margin = jnp.minimum(lengths[donor] - 1, most - lengths[sink]) // 2
    margin = jnp.where((donor == order[0]) | (sink == order[0]) | (lengths[sink] == 0), 0, jnp.maximum(margin, 0))
    passed = jax.random.randint(jax.random.fold_in(own, 4), (count // 2,), 0, 1 << 20) % (margin + 1)
    lengths = lengths.at[donor].add(-passed).at[sink].add(passed)
    items = jnp.searchsorted(jnp.cumsum(lengths), jnp.arange(rows * top), side="right").astype(jnp.int32)
    table = items.reshape(top, rows).T
    table = table[jax.random.permutation(jax.random.fold_in(own, 1), rows)]
    rotation = jax.random.randint(jax.random.fold_in(own, 2), (rows, 1), 0, top)
    return jnp.take_along_axis(table, (jnp.arange(top)[None, :] + rotation) % top, axis=1)


def shares(amount, total, limit, skew, full):
    weights = [(1 << 20) // math.isqrt(rank ** skew) + 1 for rank in range(1, amount + 1)]
    largest = limit if full else min(limit, max(-(-total // amount), total * weights[0] // sum(weights)))
    least = 1 if total - largest >= amount - 1 else 0
    given, rest = [largest] + [least] * (amount - 1), total - largest - least * (amount - 1)
    while rest > 0:
        candidates = [i for i in range(1, amount) if given[i] < largest] or [i for i in range(1, amount) if given[i] < limit]
        pool, remaining = sum([weights[i] for i in candidates]), rest
        for i in candidates:
            extra = min(limit - given[i], max(1, remaining * weights[i] // pool), rest)
            given[i] = given[i] + extra
            rest = rest - extra
    return np.array(given)


def normal_values(key, extent, width, bound, split=(), kind=jnp.bfloat16):
    entries = jax.random.normal(key, extent, jnp.float32) * width
    if len(split) > 0:
        entries = steps_of(key, extent, split, -0.22, 0.18) * entries
    return jnp.clip(entries, min=-bound, max=bound).astype(kind)


def setup_inputs(seed: int = 0) -> dict:
    keys = jax.random.split(jax.random.key(seed), 10)
    hidden_in = normal_values(keys[0], (TOKENS, D), 1.0, 6.0, ((0, 16), (1, 8)))
    context = normal_values(keys[1], (TOKENS, D), 1.0, 6.0, ((0, 16),))
    branch_wo = normal_values(keys[2], (EXPERTS, D, D), D ** -0.5, 0.09375, ((0, 8), (1, 16)))
    expert_ids_keys = jax.random.split(jax.random.fold_in(keys[3], 1), TOKENS // TOK_DEV)
    expert_ids_turns = jax.random.permutation(jax.random.fold_in(keys[3], 3), TOKENS // TOK_DEV)
    expert_ids = jax.vmap(lambda own, number: shared_out(jax.random.fold_in(keys[3], 2), own, number, TOK_DEV, EXPERTS, 2, CAP, 1))(expert_ids_keys, expert_ids_turns).reshape((TOKENS, 2))
    gate_num = plant(jax.random.randint(keys[4], (TOKENS, 2), 1, 17), jax.random.fold_in(keys[4], 1), 1, 16).astype(jnp.int32)
    w_gate = normal_values(keys[5], (EXPERTS, D, FF), D ** -0.5, 0.09375, ((0, 8), (2, 16)))
    w_up = normal_values(keys[6], (EXPERTS, D, FF), D ** -0.5, 0.09375, ((0, 8), (2, 16)))
    w_down = normal_values(keys[7], (EXPERTS, FF, D), FF ** -0.5, 0.0625, ((0, 8), (1, 16)))
    cotangent = normal_values(keys[8], (TOKENS, D), 1.0, 6.0, ((0, 16), (1, 8)))
    return dict(hidden_in=hidden_in, context=context, branch_wo=branch_wo, expert_ids=expert_ids, gate_num=gate_num, w_gate=w_gate, w_up=w_up, w_down=w_down, cotangent=cotangent)


def expert_pass(operands):
    rows_x, rows_g, weight_gate, weight_up, weight_down = operands
    gate_pre = jnp.dot(rows_x, weight_gate, preferred_element_type=jnp.float32)
    up_pre = jnp.dot(rows_x, weight_up, preferred_element_type=jnp.float32)
    sigma = jax.nn.sigmoid(gate_pre)
    silu = gate_pre * sigma
    act = (silu * up_pre).astype(jnp.bfloat16)
    d_act = jnp.dot(rows_g, weight_down.T, preferred_element_type=jnp.float32)
    d_gate = (d_act * up_pre * sigma * (1.0 + gate_pre * (1.0 - sigma))).astype(jnp.bfloat16)
    d_up = (d_act * silu).astype(jnp.bfloat16)
    grad_gate = jnp.dot(rows_x.T, d_gate, preferred_element_type=jnp.float32).astype(jnp.bfloat16)
    grad_up = jnp.dot(rows_x.T, d_up, preferred_element_type=jnp.float32).astype(jnp.bfloat16)
    grad_down = jnp.dot(act.T, rows_g, preferred_element_type=jnp.float32).astype(jnp.bfloat16)
    block_width = FF // N_DP

    def add_block(index, totals):
        start = (index * block_width).astype(jnp.int32)
        act_part = lax.dynamic_slice_in_dim(act, start, block_width, 1)
        gate_part = lax.dynamic_slice_in_dim(d_gate, start, block_width, 1)
        up_part = lax.dynamic_slice_in_dim(d_up, start, block_width, 1)
        down_part = lax.dynamic_slice_in_dim(weight_down, start, block_width, 0)
        wg_part = lax.dynamic_slice_in_dim(weight_gate, start, block_width, 1)
        wu_part = lax.dynamic_slice_in_dim(weight_up, start, block_width, 1)
        out_term = jnp.dot(act_part, down_part, preferred_element_type=jnp.float32).astype(jnp.bfloat16)
        in_term = (jnp.dot(gate_part, wg_part.T, preferred_element_type=jnp.float32)
                   + jnp.dot(up_part, wu_part.T, preferred_element_type=jnp.float32)).astype(jnp.bfloat16)
        out_term, in_term = lax.optimization_barrier((out_term, in_term))
        return (totals[0] + out_term.astype(jnp.float32), totals[1] + in_term.astype(jnp.float32))

    zeros = jnp.zeros((rows_x.shape[0], D), jnp.float32)
    out_total, in_total = lax.fori_loop(0, N_DP, add_block, (zeros, zeros))
    return (out_total.astype(jnp.bfloat16), in_total.astype(jnp.bfloat16), grad_gate, grad_up, grad_down)


def reference(hidden_in, context, branch_wo, expert_ids, gate_num, w_gate, w_up, w_down, cotangent):
    summed = jnp.sum(branch_wo.astype(jnp.float32), axis=0)
    wo_mean = (summed / EXPERTS).astype(jnp.bfloat16)
    attended = jnp.dot(context, wo_mean, preferred_element_type=jnp.float32)
    hidden = (hidden_in.astype(jnp.float32) + attended).astype(jnp.bfloat16)
    share = gate_num.astype(jnp.float32)
    share = share / jnp.sum(share, axis=1, keepdims=True)
    weighted = (share[:, :, None] * cotangent.astype(jnp.float32)[:, None, :]).astype(jnp.bfloat16)
    block_ids = expert_ids.reshape(N_DP, TOK_DEV * 2)
    labels = jnp.arange(EXPERTS, dtype=jnp.int32)
    onehot = (block_ids[:, :, None] == labels[None, None, :]).astype(jnp.int32)
    before = jnp.cumsum(onehot, axis=1) - onehot
    slot = jnp.sum(before * onehot, axis=2)
    blocks = jnp.arange(N_DP, dtype=jnp.int32)[:, None]
    where = (block_ids * (N_DP * CAP) + blocks * CAP + slot).reshape(-1).astype(jnp.int32)
    total_rows = EXPERTS * N_DP * CAP
    doubled = jnp.repeat(hidden, 2, axis=0)
    rows_x = jnp.zeros((total_rows, D), jnp.bfloat16).at[where].set(doubled)
    rows_g = jnp.zeros((total_rows, D), jnp.bfloat16).at[where].set(weighted.reshape(TOKENS * 2, D))
    rows_x = rows_x.reshape(EXPERTS, N_DP * CAP, D)
    rows_g = rows_g.reshape(EXPERTS, N_DP * CAP, D)
    expert_out, expert_dx, grad_gate, grad_up, grad_down = lax.map(expert_pass, (rows_x, rows_g, w_gate, w_up, w_down))
    out_picked = expert_out.reshape(total_rows, D)[where].reshape(TOKENS, 2, D).astype(jnp.float32)
    dx_picked = expert_dx.reshape(total_rows, D)[where].reshape(TOKENS, 2, D).astype(jnp.float32)
    mixed = (hidden.astype(jnp.float32) + jnp.sum(share[:, :, None] * out_picked, axis=1)).astype(jnp.bfloat16)
    input_grad = (cotangent.astype(jnp.float32) + jnp.sum(dx_picked, axis=1)).astype(jnp.bfloat16)
    return (mixed, input_grad, grad_gate, grad_up, grad_down)
```

```python
import jax
import jax.numpy as jnp
from jax import lax
from jax.sharding import PartitionSpec as P


def swiglu_parts(gate_pre, up_pre, d_act):
    sigma = jax.nn.sigmoid(gate_pre)
    silu = gate_pre * sigma
    act = (silu * up_pre).astype(jnp.bfloat16)
    d_gate = (d_act * up_pre * sigma * (1.0 + gate_pre * (1.0 - sigma))).astype(jnp.bfloat16)
    d_up = (d_act * silu).astype(jnp.bfloat16)
    return (act, d_gate, d_up)


def shards(hidden_in, context, branch_wo, expert_ids, gate_num, w_gate, w_up, w_down, cotangent):
    n_branch = lax.axis_size("branch")
    rows_tok, width = hidden_in.shape
    model_width = context.shape[1]
    capacity = 3 * rows_tok // n_branch
    flat_ids = expert_ids.reshape(-1)
    labels = jnp.arange(n_branch, dtype=jnp.int32)
    onehot = (flat_ids[:, None] == labels[None, :]).astype(jnp.int32)
    before = jnp.cumsum(onehot, axis=0) - onehot
    slot = flat_ids * capacity + jnp.sum(before * onehot, axis=1)
    placing = (jnp.arange(n_branch * capacity, dtype=jnp.int32)[:, None] == slot[None, :]).astype(
        jnp.bfloat16
    )
    share = gate_num.astype(jnp.float32)
    share = share / jnp.sum(share, axis=1, keepdims=True)
    weighted = (
        share.reshape(-1)[:, None] * jnp.repeat(cotangent.astype(jnp.float32), 2, axis=0)
    ).astype(jnp.bfloat16)
    send_grads = (
        jnp.dot(placing, weighted, preferred_element_type=jnp.float32)
        .astype(jnp.bfloat16)
        .reshape(n_branch, capacity, width)
    )
    got_grads = lax.all_to_all(send_grads, "branch", split_axis=0, concat_axis=2, tiled=True)
    all_grads = lax.all_gather(got_grads, "dp", axis=1, tiled=True)
    got_grads, wo_local = lax.optimization_barrier((got_grads, branch_wo[0]))
    pieces = lax.all_to_all(wo_local, "branch", split_axis=1, concat_axis=0, tiled=True)
    summed = jnp.sum(
        pieces.reshape(n_branch, -1, width).astype(jnp.float32), axis=0
    )
    mean_block = (summed / n_branch).astype(jnp.bfloat16)
    mean_block, all_grads = lax.optimization_barrier((mean_block, all_grads))
    attended = jnp.dot(
        context,
        lax.all_gather(mean_block, "dp", axis=0, tiled=True),
        preferred_element_type=jnp.float32,
    )
    hidden = (hidden_in.astype(jnp.float32) + attended).astype(jnp.bfloat16)
    doubled = jnp.repeat(hidden, 2, axis=0)
    send_rows = (
        jnp.dot(placing, doubled, preferred_element_type=jnp.float32)
        .astype(jnp.bfloat16)
        .reshape(n_branch, capacity, width)
    )
    weight_gate = w_gate[0]
    weight_up = w_up[0]
    weight_down = w_down[0]
    got_rows = lax.all_to_all(send_rows, "branch", split_axis=0, concat_axis=2, tiled=True)
    all_rows = lax.all_gather(got_rows, "dp", axis=1, tiled=True)
    rows_two = all_rows[0]
    grads_two = all_grads[0]
    gate_pre = jnp.dot(rows_two, weight_gate, preferred_element_type=jnp.float32)
    up_pre = jnp.dot(rows_two, weight_up, preferred_element_type=jnp.float32)
    d_act = jnp.einsum("rd,fd->rf", grads_two, weight_down, preferred_element_type=jnp.float32)
    act, d_gate, d_up = swiglu_parts(gate_pre, up_pre, d_act)
    grad_gate = jnp.einsum("rd,rf->df", rows_two, d_gate, preferred_element_type=jnp.float32)
    grad_up = jnp.einsum("rd,rf->df", rows_two, d_up, preferred_element_type=jnp.float32)
    grad_down = jnp.einsum("rf,rd->fd", act, grads_two, preferred_element_type=jnp.float32)
    output_term = jnp.dot(act, weight_down, preferred_element_type=jnp.float32)
    input_term = jnp.einsum(
        "rf,df->rd", d_gate, weight_gate, preferred_element_type=jnp.float32
    ) + jnp.einsum("rf,df->rd", d_up, weight_up, preferred_element_type=jnp.float32)
    folded = lax.psum_scatter(
        jnp.concatenate([output_term, input_term], axis=1).astype(jnp.bfloat16),
        "dp",
        scatter_dimension=0,
        tiled=True,
    )
    packed = folded.reshape(1, capacity, 2, model_width)
    returned = lax.all_to_all(packed, "branch", split_axis=3, concat_axis=0, tiled=True)
    picked = jnp.einsum(
        "sr,sc->rc",
        placing,
        returned.reshape(n_branch * capacity, 2 * width),
        preferred_element_type=jnp.float32,
    )
    picked = picked.reshape(rows_tok, 2, 2, width)
    mixed = (
        hidden.astype(jnp.float32) + jnp.sum(share[:, :, None] * picked[:, :, 0], axis=1)
    ).astype(jnp.bfloat16)
    input_grad = (cotangent.astype(jnp.float32) + jnp.sum(picked[:, :, 1], axis=1)).astype(
        jnp.bfloat16
    )
    return (
        mixed,
        input_grad,
        grad_gate.astype(jnp.bfloat16)[None],
        grad_up.astype(jnp.bfloat16)[None],
        grad_down.astype(jnp.bfloat16)[None],
    )


def solution(mesh):
    return jax.shard_map(
        shards,
        mesh=mesh,
        in_specs=(
            P("dp", "branch"),
            P("dp", None),
            P("branch", "dp", None),
            P("dp", None),
            P("dp", None),
            P("branch", None, "dp"),
            P("branch", None, "dp"),
            P("branch", "dp", None),
            P("dp", "branch"),
        ),
        out_specs=(
            P("dp", "branch"),
            P("dp", "branch"),
            P("branch", None, "dp"),
            P("branch", None, "dp"),
            P("branch", "dp", None),
        ),
        check_vma=False,
    )
```

```python
import jax
import jax.numpy as jnp
from jax import lax
from jax.sharding import Mesh, PartitionSpec as P

DP = ("dpo", "core")


def swiglu_parts(gate_pre, up_pre, d_act):
    sigma = jax.nn.sigmoid(gate_pre)
    silu = gate_pre * sigma
    act = (silu * up_pre).astype(jnp.bfloat16)
    d_gate = (d_act * up_pre * sigma * (1.0 + gate_pre * (1.0 - sigma))).astype(jnp.bfloat16)
    d_up = (d_act * silu).astype(jnp.bfloat16)
    return (act, d_gate, d_up)


def shards(hidden_in, context, branch_wo, expert_ids, gate_num, w_gate, w_up, w_down, cotangent):
    n_branch = lax.axis_size("branch")
    rows_tok, width = hidden_in.shape
    model_width = context.shape[1]
    capacity = 3 * rows_tok // n_branch
    flat_ids = expert_ids.reshape(-1)
    labels = jnp.arange(n_branch, dtype=jnp.int32)
    onehot = (flat_ids[:, None] == labels[None, :]).astype(jnp.int32)
    before = jnp.cumsum(onehot, axis=0) - onehot
    slot = flat_ids * capacity + jnp.sum(before * onehot, axis=1)
    placing = (jnp.arange(n_branch * capacity, dtype=jnp.int32)[:, None] == slot[None, :]).astype(
        jnp.bfloat16
    )
    share = gate_num.astype(jnp.float32)
    share = share / jnp.sum(share, axis=1, keepdims=True)
    weighted = (
        share.reshape(-1)[:, None] * jnp.repeat(cotangent.astype(jnp.float32), 2, axis=0)
    ).astype(jnp.bfloat16)
    send_grads = (
        jnp.dot(placing, weighted, preferred_element_type=jnp.float32)
        .astype(jnp.bfloat16)
        .reshape(n_branch, capacity, width)
    )
    got_grads = lax.all_to_all(send_grads, "branch", split_axis=0, concat_axis=2, tiled=True)
    all_grads = lax.all_gather(got_grads, DP, axis=1, tiled=True)
    got_grads, wo_local = lax.optimization_barrier((got_grads, branch_wo[0]))
    pieces = lax.all_to_all(wo_local, "branch", split_axis=1, concat_axis=0, tiled=True)
    summed = jnp.sum(
        pieces.reshape(n_branch, -1, width).astype(jnp.float32), axis=0
    )
    mean_block = (summed / n_branch).astype(jnp.bfloat16)
    mean_block, all_grads = lax.optimization_barrier((mean_block, all_grads))
    attended = jnp.dot(
        context,
        lax.all_gather(mean_block, DP, axis=0, tiled=True),
        preferred_element_type=jnp.float32,
    )
    hidden = (hidden_in.astype(jnp.float32) + attended).astype(jnp.bfloat16)
    doubled = jnp.repeat(hidden, 2, axis=0)
    send_rows = (
        jnp.dot(placing, doubled, preferred_element_type=jnp.float32)
        .astype(jnp.bfloat16)
        .reshape(n_branch, capacity, width)
    )
    weight_gate = w_gate[0]
    weight_up = w_up[0]
    weight_down = w_down[0]
    got_rows = lax.all_to_all(send_rows, "branch", split_axis=0, concat_axis=2, tiled=True)
    all_rows = lax.all_gather(got_rows, DP, axis=1, tiled=True)
    rows_two = all_rows[0]
    grads_two = all_grads[0]
    gate_pre = jnp.dot(rows_two, weight_gate, preferred_element_type=jnp.float32)
    up_pre = jnp.dot(rows_two, weight_up, preferred_element_type=jnp.float32)
    d_act = jnp.einsum("rd,fd->rf", grads_two, weight_down, preferred_element_type=jnp.float32)
    act, d_gate, d_up = swiglu_parts(gate_pre, up_pre, d_act)
    grad_gate = jnp.einsum("rd,rf->df", rows_two, d_gate, preferred_element_type=jnp.float32)
    grad_up = jnp.einsum("rd,rf->df", rows_two, d_up, preferred_element_type=jnp.float32)
    grad_down = jnp.einsum("rf,rd->fd", act, grads_two, preferred_element_type=jnp.float32)
    output_term = jnp.dot(act, weight_down, preferred_element_type=jnp.float32)
    input_term = jnp.einsum(
        "rf,df->rd", d_gate, weight_gate, preferred_element_type=jnp.float32
    ) + jnp.einsum("rf,df->rd", d_up, weight_up, preferred_element_type=jnp.float32)
    both = jnp.concatenate([output_term, input_term], axis=1).astype(jnp.bfloat16)
    both = both.reshape(-1, 2, capacity, 2 * model_width)
    core = lax.axis_index("core")
    mine = lax.dynamic_index_in_dim(both, core, axis=1, keepdims=False)
    other = lax.dynamic_index_in_dim(both, 1 - core, axis=1, keepdims=False)
    partner = lax.ppermute(other, "core", perm=[(0, 1), (1, 0)])
    paired = (mine.astype(jnp.float32) + partner.astype(jnp.float32)).astype(jnp.bfloat16)
    folded = lax.psum_scatter(
        paired.reshape(-1, 2 * model_width),
        "dpo",
        scatter_dimension=0,
        tiled=True,
    )
    packed = folded.reshape(1, capacity, 2, model_width)
    returned = lax.all_to_all(packed, "branch", split_axis=3, concat_axis=0, tiled=True)
    picked = jnp.einsum(
        "sr,sc->rc",
        placing,
        returned.reshape(n_branch * capacity, 2 * width),
        preferred_element_type=jnp.float32,
    )
    picked = picked.reshape(rows_tok, 2, 2, width)
    mixed = (
        hidden.astype(jnp.float32) + jnp.sum(share[:, :, None] * picked[:, :, 0], axis=1)
    ).astype(jnp.bfloat16)
    input_grad = (cotangent.astype(jnp.float32) + jnp.sum(picked[:, :, 1], axis=1)).astype(
        jnp.bfloat16
    )
    return (
        mixed,
        input_grad,
        grad_gate.astype(jnp.bfloat16)[None],
        grad_up.astype(jnp.bfloat16)[None],
        grad_down.astype(jnp.bfloat16)[None],
    )


def solution(mesh):
    split = Mesh(
        mesh.devices.reshape(mesh.shape["branch"], mesh.shape["dp"] // 2, 2),
        ("branch", "dpo", "core"),
    )
    return jax.shard_map(
        shards,
        mesh=split,
        in_specs=(
            P(DP, "branch"),
            P(DP, None),
            P("branch", DP, None),
            P(DP, None),
            P(DP, None),
            P("branch", None, DP),
            P("branch", None, DP),
            P("branch", DP, None),
            P(DP, "branch"),
        ),
        out_specs=(
            P(DP, "branch"),
            P(DP, "branch"),
            P("branch", None, DP),
            P("branch", None, DP),
            P("branch", DP, None),
        ),
        check_vma=False,
    )
```

```python
import jax
import jax.numpy as jnp
from jax import lax
from jax.sharding import PartitionSpec as P


def swiglu_parts(gate_pre, up_pre, d_act):
    sigma = jax.nn.sigmoid(gate_pre)
    silu = gate_pre * sigma
    act = (silu * up_pre).astype(jnp.bfloat16)
    d_gate = (d_act * up_pre * sigma * (1.0 + gate_pre * (1.0 - sigma))).astype(jnp.bfloat16)
    d_up = (d_act * silu).astype(jnp.bfloat16)
    return (act, d_gate, d_up)


def shards(hidden_in, context, branch_wo, expert_ids, gate_num, w_gate, w_up, w_down, cotangent):
    n_branch = lax.axis_size("branch")
    rows_tok, width = hidden_in.shape
    model_width = context.shape[1]
    capacity = 3 * rows_tok // n_branch
    flat_ids = expert_ids.reshape(-1)
    labels = jnp.arange(n_branch, dtype=jnp.int32)
    onehot = (flat_ids[:, None] == labels[None, :]).astype(jnp.int32)
    before = jnp.cumsum(onehot, axis=0) - onehot
    slot = flat_ids * capacity + jnp.sum(before * onehot, axis=1)
    placing = (jnp.arange(n_branch * capacity, dtype=jnp.int32)[:, None] == slot[None, :]).astype(
        jnp.bfloat16
    )
    share = gate_num.astype(jnp.float32)
    share = share / jnp.sum(share, axis=1, keepdims=True)
    weighted = (
        share.reshape(-1)[:, None] * jnp.repeat(cotangent.astype(jnp.float32), 2, axis=0)
    ).astype(jnp.bfloat16)
    send_grads = (
        jnp.dot(placing, weighted, preferred_element_type=jnp.float32)
        .astype(jnp.bfloat16)
        .reshape(n_branch, capacity, width)
    )
    got_grads = lax.all_to_all(send_grads, "branch", split_axis=0, concat_axis=2, tiled=True)
    all_grads = lax.all_gather(got_grads, "dp", axis=1, tiled=True)
    got_grads, wo_local = lax.optimization_barrier((got_grads, branch_wo[0]))
    pieces = lax.all_to_all(wo_local, "branch", split_axis=1, concat_axis=0, tiled=True)
    summed = jnp.sum(
        pieces.reshape(n_branch, -1, width).astype(jnp.float32), axis=0
    )
    mean_block = (summed / n_branch).astype(jnp.bfloat16)
    mean_block, all_grads = lax.optimization_barrier((mean_block, all_grads))
    attended = jnp.dot(
        context,
        lax.all_gather(mean_block, "dp", axis=0, tiled=True),
        preferred_element_type=jnp.float32,
    )
    hidden = (hidden_in.astype(jnp.float32) + attended).astype(jnp.bfloat16)
    doubled = jnp.repeat(hidden, 2, axis=0)
    send_rows = (
        jnp.dot(placing, doubled, preferred_element_type=jnp.float32)
        .astype(jnp.bfloat16)
        .reshape(n_branch, capacity, width)
    )
    weight_gate = w_gate[0]
    weight_up = w_up[0]
    weight_down = w_down[0]
    got_rows = lax.all_to_all(send_rows, "branch", split_axis=0, concat_axis=2, tiled=True)
    all_rows = lax.all_gather(got_rows, "dp", axis=1, tiled=True)
    rows_two = all_rows[0]
    grads_two = all_grads[0]
    gate_pre = jnp.dot(rows_two, weight_gate, preferred_element_type=jnp.float32)
    up_pre = jnp.dot(rows_two, weight_up, preferred_element_type=jnp.float32)
    d_act = jnp.einsum("rd,fd->rf", grads_two, weight_down, preferred_element_type=jnp.float32)
    act, d_gate, d_up = swiglu_parts(gate_pre, up_pre, d_act)
    grad_gate = jnp.einsum("rd,rf->df", rows_two, d_gate, preferred_element_type=jnp.float32)
    grad_up = jnp.einsum("rd,rf->df", rows_two, d_up, preferred_element_type=jnp.float32)
    grad_down = jnp.einsum("rf,rd->fd", act, grads_two, preferred_element_type=jnp.float32)
    output_term = jnp.dot(act, weight_down, preferred_element_type=jnp.float32)
    input_term = jnp.einsum(
        "rf,df->rd", d_gate, weight_gate, preferred_element_type=jnp.float32
    ) + jnp.einsum("rf,df->rd", d_up, weight_up, preferred_element_type=jnp.float32)
    out_part = lax.psum_scatter(
        output_term.astype(jnp.bfloat16), "dp", scatter_dimension=0, tiled=True
    )
    in_part = lax.psum_scatter(
        input_term.astype(jnp.bfloat16), "dp", scatter_dimension=0, tiled=True
    )
    packed = jnp.stack([out_part, in_part], axis=1)[None]
    returned = lax.all_to_all(packed, "branch", split_axis=3, concat_axis=0, tiled=True)
    picked = jnp.einsum(
        "sr,sc->rc",
        placing,
        returned.reshape(n_branch * capacity, 2 * width),
        preferred_element_type=jnp.float32,
    )
    picked = picked.reshape(rows_tok, 2, 2, width)
    mixed = (
        hidden.astype(jnp.float32) + jnp.sum(share[:, :, None] * picked[:, :, 0], axis=1)
    ).astype(jnp.bfloat16)
    input_grad = (cotangent.astype(jnp.float32) + jnp.sum(picked[:, :, 1], axis=1)).astype(
        jnp.bfloat16
    )
    return (
        mixed,
        input_grad,
        grad_gate.astype(jnp.bfloat16)[None],
        grad_up.astype(jnp.bfloat16)[None],
        grad_down.astype(jnp.bfloat16)[None],
    )


def solution(mesh):
    return jax.shard_map(
        shards,
        mesh=mesh,
        in_specs=(
            P("dp", "branch"),
            P("dp", None),
            P("branch", "dp", None),
            P("dp", None),
            P("dp", None),
            P("branch", None, "dp"),
            P("branch", None, "dp"),
            P("branch", "dp", None),
            P("dp", "branch"),
        ),
        out_specs=(
            P("dp", "branch"),
            P("dp", "branch"),
            P("branch", None, "dp"),
            P("branch", None, "dp"),
            P("branch", "dp", None),
        ),
        check_vma=False,
    )
```

```python
import jax
import jax.numpy as jnp
from jax import lax
from jax.sharding import PartitionSpec as P


def swiglu_parts(gate_pre, up_pre, d_act):
    sigma = jax.nn.sigmoid(gate_pre)
    silu = gate_pre * sigma
    act = (silu * up_pre).astype(jnp.bfloat16)
    d_gate = (d_act * up_pre * sigma * (1.0 + gate_pre * (1.0 - sigma))).astype(jnp.bfloat16)
    d_up = (d_act * silu).astype(jnp.bfloat16)
    return (act, d_gate, d_up)


def shards(hidden_in, context, branch_wo, expert_ids, gate_num, w_gate, w_up, w_down, cotangent):
    n_branch = lax.axis_size("branch")
    rows_tok, width = hidden_in.shape
    model_width = context.shape[1]
    capacity = 3 * rows_tok // n_branch
    flat_ids = expert_ids.reshape(-1)
    labels = jnp.arange(n_branch, dtype=jnp.int32)
    onehot = (flat_ids[:, None] == labels[None, :]).astype(jnp.int32)
    before = jnp.cumsum(onehot, axis=0) - onehot
    slot = flat_ids * capacity + jnp.sum(before * onehot, axis=1)
    placing = (jnp.arange(n_branch * capacity, dtype=jnp.int32)[:, None] == slot[None, :]).astype(
        jnp.bfloat16
    )
    share = gate_num.astype(jnp.float32)
    share = share / jnp.sum(share, axis=1, keepdims=True)
    weighted = (
        share.reshape(-1)[:, None] * jnp.repeat(cotangent.astype(jnp.float32), 2, axis=0)
    ).astype(jnp.bfloat16)
    send_grads = (
        jnp.dot(placing, weighted, preferred_element_type=jnp.float32)
        .astype(jnp.bfloat16)
        .reshape(n_branch, capacity, width)
    )
    got_grads = lax.all_to_all(send_grads, "branch", split_axis=0, concat_axis=2, tiled=True)
    all_grads = lax.all_gather(got_grads, "dp", axis=1, tiled=True)
    got_grads, wo_local = lax.optimization_barrier((got_grads, branch_wo[0]))
    me = lax.axis_index("branch")
    summed = lax.dynamic_slice_in_dim(wo_local, me * width, width, axis=1).astype(jnp.float32)
    for k in range(1, n_branch):
        piece = lax.dynamic_slice_in_dim(wo_local, ((me + k) % n_branch) * width, width, axis=1)
        got = lax.ppermute(piece, "branch", perm=[(i, (i + k) % n_branch) for i in range(n_branch)])
        summed = summed + got.astype(jnp.float32)
    mean_block = (summed / n_branch).astype(jnp.bfloat16)
    mean_block, all_grads = lax.optimization_barrier((mean_block, all_grads))
    attended = jnp.dot(
        context,
        lax.all_gather(mean_block, "dp", axis=0, tiled=True),
        preferred_element_type=jnp.float32,
    )
    hidden = (hidden_in.astype(jnp.float32) + attended).astype(jnp.bfloat16)
    doubled = jnp.repeat(hidden, 2, axis=0)
    send_rows = (
        jnp.dot(placing, doubled, preferred_element_type=jnp.float32)
        .astype(jnp.bfloat16)
        .reshape(n_branch, capacity, width)
    )
    weight_gate = w_gate[0]
    weight_up = w_up[0]
    weight_down = w_down[0]
    got_rows = lax.all_to_all(send_rows, "branch", split_axis=0, concat_axis=2, tiled=True)
    all_rows = lax.all_gather(got_rows, "dp", axis=1, tiled=True)
    rows_two = all_rows[0]
    grads_two = all_grads[0]
    gate_pre = jnp.dot(rows_two, weight_gate, preferred_element_type=jnp.float32)
    up_pre = jnp.dot(rows_two, weight_up, preferred_element_type=jnp.float32)
    d_act = jnp.einsum("rd,fd->rf", grads_two, weight_down, preferred_element_type=jnp.float32)
    act, d_gate, d_up = swiglu_parts(gate_pre, up_pre, d_act)
    grad_gate = jnp.einsum("rd,rf->df", rows_two, d_gate, preferred_element_type=jnp.float32)
    grad_up = jnp.einsum("rd,rf->df", rows_two, d_up, preferred_element_type=jnp.float32)
    grad_down = jnp.einsum("rf,rd->fd", act, grads_two, preferred_element_type=jnp.float32)
    output_term = jnp.dot(act, weight_down, preferred_element_type=jnp.float32)
    input_term = jnp.einsum(
        "rf,df->rd", d_gate, weight_gate, preferred_element_type=jnp.float32
    ) + jnp.einsum("rf,df->rd", d_up, weight_up, preferred_element_type=jnp.float32)
    folded = lax.psum_scatter(
        jnp.concatenate([output_term, input_term], axis=1).astype(jnp.bfloat16),
        "dp",
        scatter_dimension=0,
        tiled=True,
    )
    packed = folded.reshape(1, capacity, 2, model_width)
    returned = lax.all_to_all(packed, "branch", split_axis=3, concat_axis=0, tiled=True)
    picked = jnp.einsum(
        "sr,sc->rc",
        placing,
        returned.reshape(n_branch * capacity, 2 * width),
        preferred_element_type=jnp.float32,
    )
    picked = picked.reshape(rows_tok, 2, 2, width)
    mixed = (
        hidden.astype(jnp.float32) + jnp.sum(share[:, :, None] * picked[:, :, 0], axis=1)
    ).astype(jnp.bfloat16)
    input_grad = (cotangent.astype(jnp.float32) + jnp.sum(picked[:, :, 1], axis=1)).astype(
        jnp.bfloat16
    )
    return (
        mixed,
        input_grad,
        grad_gate.astype(jnp.bfloat16)[None],
        grad_up.astype(jnp.bfloat16)[None],
        grad_down.astype(jnp.bfloat16)[None],
    )


def solution(mesh):
    return jax.shard_map(
        shards,
        mesh=mesh,
        in_specs=(
            P("dp", "branch"),
            P("dp", None),
            P("branch", "dp", None),
            P("dp", None),
            P("dp", None),
            P("branch", None, "dp"),
            P("branch", None, "dp"),
            P("branch", "dp", None),
            P("dp", "branch"),
        ),
        out_specs=(
            P("dp", "branch"),
            P("dp", "branch"),
            P("branch", None, "dp"),
            P("branch", None, "dp"),
            P("branch", "dp", None),
        ),
        check_vma=False,
    )
```

```python
import jax
import jax.numpy as jnp
from jax import lax
from jax.sharding import PartitionSpec as P


def swiglu_parts(gate_pre, up_pre, d_act):
    sigma = jax.nn.sigmoid(gate_pre)
    silu = gate_pre * sigma
    act = (silu * up_pre).astype(jnp.bfloat16)
    d_gate = (d_act * up_pre * sigma * (1.0 + gate_pre * (1.0 - sigma))).astype(jnp.bfloat16)
    d_up = (d_act * silu).astype(jnp.bfloat16)
    return (act, d_gate, d_up)


def dispatch(send, me):
    n = send.shape[0]
    pieces = [lax.dynamic_index_in_dim(send, me, axis=0, keepdims=False)]
    for k in range(1, n):
        piece = lax.dynamic_index_in_dim(send, (me + k) % n, axis=0, keepdims=False)
        pieces.append(lax.ppermute(piece, "branch", perm=[(i, (i + k) % n) for i in range(n)]))
    stacked = jnp.stack(pieces)
    cols = jnp.take(stacked, (me - jnp.arange(n)) % n, axis=0)
    return cols.transpose(1, 0, 2).reshape(1, send.shape[1], n * send.shape[2])


def shards(hidden_in, context, branch_wo, expert_ids, gate_num, w_gate, w_up, w_down, cotangent):
    n_branch = lax.axis_size("branch")
    rows_tok, width = hidden_in.shape
    model_width = context.shape[1]
    capacity = 3 * rows_tok // n_branch
    flat_ids = expert_ids.reshape(-1)
    labels = jnp.arange(n_branch, dtype=jnp.int32)
    onehot = (flat_ids[:, None] == labels[None, :]).astype(jnp.int32)
    before = jnp.cumsum(onehot, axis=0) - onehot
    slot = flat_ids * capacity + jnp.sum(before * onehot, axis=1)
    placing = (jnp.arange(n_branch * capacity, dtype=jnp.int32)[:, None] == slot[None, :]).astype(
        jnp.bfloat16
    )
    share = gate_num.astype(jnp.float32)
    share = share / jnp.sum(share, axis=1, keepdims=True)
    weighted = (
        share.reshape(-1)[:, None] * jnp.repeat(cotangent.astype(jnp.float32), 2, axis=0)
    ).astype(jnp.bfloat16)
    send_grads = (
        jnp.dot(placing, weighted, preferred_element_type=jnp.float32)
        .astype(jnp.bfloat16)
        .reshape(n_branch, capacity, width)
    )
    me = lax.axis_index("branch")
    wo_local = branch_wo[0]
    got_grads = dispatch(send_grads, me)
    all_grads = lax.all_gather(got_grads, "dp", axis=1, tiled=True)
    summed = lax.dynamic_slice_in_dim(wo_local, me * width, width, axis=1).astype(jnp.float32)
    for k in range(1, n_branch):
        piece = lax.dynamic_slice_in_dim(wo_local, ((me + k) % n_branch) * width, width, axis=1)
        got = lax.ppermute(piece, "branch", perm=[(i, (i + k) % n_branch) for i in range(n_branch)])
        summed = summed + got.astype(jnp.float32)
    mean_block = (summed / n_branch).astype(jnp.bfloat16)
    mean_block, all_grads = lax.optimization_barrier((mean_block, all_grads))
    attended = jnp.dot(
        context,
        lax.all_gather(mean_block, "dp", axis=0, tiled=True),
        preferred_element_type=jnp.float32,
    )
    hidden = (hidden_in.astype(jnp.float32) + attended).astype(jnp.bfloat16)
    doubled = jnp.repeat(hidden, 2, axis=0)
    send_rows = (
        jnp.dot(placing, doubled, preferred_element_type=jnp.float32)
        .astype(jnp.bfloat16)
        .reshape(n_branch, capacity, width)
    )
    weight_gate = w_gate[0]
    weight_up = w_up[0]
    weight_down = w_down[0]
    got_rows = dispatch(send_rows, me)
    all_rows = lax.all_gather(got_rows, "dp", axis=1, tiled=True)
    rows_two = all_rows[0]
    grads_two = all_grads[0]
    gate_pre = jnp.dot(rows_two, weight_gate, preferred_element_type=jnp.float32)
    up_pre = jnp.dot(rows_two, weight_up, preferred_element_type=jnp.float32)
    d_act = jnp.einsum("rd,fd->rf", grads_two, weight_down, preferred_element_type=jnp.float32)
    act, d_gate, d_up = swiglu_parts(gate_pre, up_pre, d_act)
    grad_gate = jnp.einsum("rd,rf->df", rows_two, d_gate, preferred_element_type=jnp.float32)
    grad_up = jnp.einsum("rd,rf->df", rows_two, d_up, preferred_element_type=jnp.float32)
    grad_down = jnp.einsum("rf,rd->fd", act, grads_two, preferred_element_type=jnp.float32)
    output_term = jnp.dot(act, weight_down, preferred_element_type=jnp.float32)
    input_term = jnp.einsum(
        "rf,df->rd", d_gate, weight_gate, preferred_element_type=jnp.float32
    ) + jnp.einsum("rf,df->rd", d_up, weight_up, preferred_element_type=jnp.float32)
    folded = lax.psum_scatter(
        jnp.concatenate([output_term, input_term], axis=1).astype(jnp.bfloat16),
        "dp",
        scatter_dimension=0,
        tiled=True,
    )
    packed = folded.reshape(1, capacity, 2, model_width)
    returned = lax.all_to_all(packed, "branch", split_axis=3, concat_axis=0, tiled=True)
    picked = jnp.einsum(
        "sr,sc->rc",
        placing,
        returned.reshape(n_branch * capacity, 2 * width),
        preferred_element_type=jnp.float32,
    )
    picked = picked.reshape(rows_tok, 2, 2, width)
    mixed = (
        hidden.astype(jnp.float32) + jnp.sum(share[:, :, None] * picked[:, :, 0], axis=1)
    ).astype(jnp.bfloat16)
    input_grad = (cotangent.astype(jnp.float32) + jnp.sum(picked[:, :, 1], axis=1)).astype(
        jnp.bfloat16
    )
    return (
        mixed,
        input_grad,
        grad_gate.astype(jnp.bfloat16)[None],
        grad_up.astype(jnp.bfloat16)[None],
        grad_down.astype(jnp.bfloat16)[None],
    )


def solution(mesh):
    return jax.shard_map(
        shards,
        mesh=mesh,
        in_specs=(
            P("dp", "branch"),
            P("dp", None),
            P("branch", "dp", None),
            P("dp", None),
            P("dp", None),
            P("branch", None, "dp"),
            P("branch", None, "dp"),
            P("branch", "dp", None),
            P("dp", "branch"),
        ),
        out_specs=(
            P("dp", "branch"),
            P("dp", "branch"),
            P("branch", None, "dp"),
            P("branch", None, "dp"),
            P("branch", "dp", None),
        ),
        check_vma=False,
    )
```

```python
import jax
import jax.numpy as jnp
from jax import lax
from jax.sharding import PartitionSpec as P


def swiglu_parts(gate_pre, up_pre, d_act):
    sigma = jax.nn.sigmoid(gate_pre)
    silu = gate_pre * sigma
    act = (silu * up_pre).astype(jnp.bfloat16)
    d_gate = (d_act * up_pre * sigma * (1.0 + gate_pre * (1.0 - sigma))).astype(jnp.bfloat16)
    d_up = (d_act * silu).astype(jnp.bfloat16)
    return (act, d_gate, d_up)


def shards(hidden_in, context, branch_wo, expert_ids, gate_num, w_gate, w_up, w_down, cotangent):
    n_branch = lax.axis_size("branch")
    rows_tok, width = hidden_in.shape
    model_width = context.shape[1]
    capacity = 3 * rows_tok // n_branch
    flat_ids = expert_ids.reshape(-1)
    labels = jnp.arange(n_branch, dtype=jnp.int32)
    onehot = (flat_ids[:, None] == labels[None, :]).astype(jnp.int32)
    before = jnp.cumsum(onehot, axis=0) - onehot
    slot = flat_ids * capacity + jnp.sum(before * onehot, axis=1)
    placing = (jnp.arange(n_branch * capacity, dtype=jnp.int32)[:, None] == slot[None, :]).astype(
        jnp.bfloat16
    )
    share = gate_num.astype(jnp.float32)
    share = share / jnp.sum(share, axis=1, keepdims=True)
    weighted = (
        share.reshape(-1)[:, None] * jnp.repeat(cotangent.astype(jnp.float32), 2, axis=0)
    ).astype(jnp.bfloat16)
    send_grads = (
        jnp.dot(placing, weighted, preferred_element_type=jnp.float32)
        .astype(jnp.bfloat16)
        .reshape(n_branch, capacity, width)
    )
    got_grads = lax.all_to_all(send_grads, "branch", split_axis=0, concat_axis=2, tiled=True)
    all_grads = lax.all_gather(got_grads, "dp", axis=1, tiled=True)
    got_grads, wo_local = lax.optimization_barrier((got_grads, branch_wo[0]))
    pieces = lax.all_to_all(wo_local, "branch", split_axis=1, concat_axis=0, tiled=True)
    summed = jnp.sum(
        pieces.reshape(n_branch, -1, width).astype(jnp.float32), axis=0
    )
    mean_block = (summed / n_branch).astype(jnp.bfloat16)
    mean_block, all_grads = lax.optimization_barrier((mean_block, all_grads))
    attended = jnp.dot(
        context,
        lax.all_gather(mean_block, "dp", axis=0, tiled=True),
        preferred_element_type=jnp.float32,
    )
    hidden = (hidden_in.astype(jnp.float32) + attended).astype(jnp.bfloat16)
    doubled = jnp.repeat(hidden, 2, axis=0)
    send_rows = (
        jnp.dot(placing, doubled, preferred_element_type=jnp.float32)
        .astype(jnp.bfloat16)
        .reshape(n_branch, capacity, width)
    )
    weight_gate = w_gate[0]
    weight_up = w_up[0]
    weight_down = w_down[0]
    got_rows = lax.all_to_all(send_rows, "branch", split_axis=0, concat_axis=2, tiled=True)
    all_rows = lax.all_gather(got_rows, "dp", axis=1, tiled=True)
    rows_two = all_rows[0]
    grads_two = all_grads[0]
    gate_pre = jnp.dot(rows_two, weight_gate, preferred_element_type=jnp.float32)
    up_pre = jnp.dot(rows_two, weight_up, preferred_element_type=jnp.float32)
    d_act = jnp.einsum("rd,fd->rf", grads_two, weight_down, preferred_element_type=jnp.float32)
    act, d_gate, d_up = swiglu_parts(gate_pre, up_pre, d_act)
    grad_gate = jnp.einsum("rd,rf->df", rows_two, d_gate, preferred_element_type=jnp.float32)
    grad_up = jnp.einsum("rd,rf->df", rows_two, d_up, preferred_element_type=jnp.float32)
    grad_down = jnp.einsum("rf,rd->fd", act, grads_two, preferred_element_type=jnp.float32)
    output_term = jnp.dot(act, weight_down, preferred_element_type=jnp.float32)
    input_term = jnp.einsum(
        "rf,df->rd", d_gate, weight_gate, preferred_element_type=jnp.float32
    ) + jnp.einsum("rf,df->rd", d_up, weight_up, preferred_element_type=jnp.float32)
    both = jnp.stack(
        [
            output_term.astype(jnp.bfloat16).reshape(-1, n_branch, width),
            input_term.astype(jnp.bfloat16).reshape(-1, n_branch, width),
        ],
        axis=2,
    )
    folded = lax.psum_scatter(
        both.reshape(-1, 2 * model_width), "dp", scatter_dimension=0, tiled=True
    )
    packed = folded.reshape(capacity, n_branch, 2 * width).transpose(1, 0, 2)
    returned = lax.all_to_all(packed, "branch", split_axis=0, concat_axis=0, tiled=True)
    picked = jnp.einsum(
        "sr,sc->rc",
        placing,
        returned.reshape(n_branch * capacity, 2 * width),
        preferred_element_type=jnp.float32,
    )
    picked = picked.reshape(rows_tok, 2, 2, width)
    mixed = (
        hidden.astype(jnp.float32) + jnp.sum(share[:, :, None] * picked[:, :, 0], axis=1)
    ).astype(jnp.bfloat16)
    input_grad = (cotangent.astype(jnp.float32) + jnp.sum(picked[:, :, 1], axis=1)).astype(
        jnp.bfloat16
    )
    return (
        mixed,
        input_grad,
        grad_gate.astype(jnp.bfloat16)[None],
        grad_up.astype(jnp.bfloat16)[None],
        grad_down.astype(jnp.bfloat16)[None],
    )


def solution(mesh):
    return jax.shard_map(
        shards,
        mesh=mesh,
        in_specs=(
            P("dp", "branch"),
            P("dp", None),
            P("branch", "dp", None),
            P("dp", None),
            P("dp", None),
            P("branch", None, "dp"),
            P("branch", None, "dp"),
            P("branch", "dp", None),
            P("dp", "branch"),
        ),
        out_specs=(
            P("dp", "branch"),
            P("dp", "branch"),
            P("branch", None, "dp"),
            P("branch", None, "dp"),
            P("branch", "dp", None),
        ),
        check_vma=False,
    )
```

```python
import jax
import jax.numpy as jnp
from jax import lax
from jax.sharding import PartitionSpec as P


def swiglu_parts(gate_pre, up_pre, d_act):
    sigma = jax.nn.sigmoid(gate_pre)
    silu = gate_pre * sigma
    act = (silu * up_pre).astype(jnp.bfloat16)
    d_gate = (d_act * up_pre * sigma * (1.0 + gate_pre * (1.0 - sigma))).astype(jnp.bfloat16)
    d_up = (d_act * silu).astype(jnp.bfloat16)
    return (act, d_gate, d_up)


def shards(hidden_in, context, branch_wo, expert_ids, gate_num, w_gate, w_up, w_down, cotangent):
    n_branch = lax.axis_size("branch")
    rows_tok, width = hidden_in.shape
    model_width = context.shape[1]
    capacity = 3 * rows_tok // n_branch
    flat_ids = expert_ids.reshape(-1)
    labels = jnp.arange(n_branch, dtype=jnp.int32)
    onehot = (flat_ids[:, None] == labels[None, :]).astype(jnp.int32)
    before = jnp.cumsum(onehot, axis=0) - onehot
    slot = flat_ids * capacity + jnp.sum(before * onehot, axis=1)
    placing = (jnp.arange(n_branch * capacity, dtype=jnp.int32)[:, None] == slot[None, :]).astype(
        jnp.bfloat16
    )
    share = gate_num.astype(jnp.float32)
    share = share / jnp.sum(share, axis=1, keepdims=True)
    weighted = (
        share.reshape(-1)[:, None] * jnp.repeat(cotangent.astype(jnp.float32), 2, axis=0)
    ).astype(jnp.bfloat16)
    send_grads = (
        jnp.dot(placing, weighted, preferred_element_type=jnp.float32)
        .astype(jnp.bfloat16)
        .reshape(n_branch, capacity, width)
    )
    got_grads = lax.all_to_all(send_grads, "branch", split_axis=0, concat_axis=2, tiled=True)
    all_grads = lax.all_gather(got_grads, "dp", axis=1, tiled=True)
    got_grads, wo_local = lax.optimization_barrier((got_grads, branch_wo[0]))
    pieces = lax.all_to_all(wo_local, "branch", split_axis=1, concat_axis=0, tiled=True)
    summed = jnp.sum(
        pieces.reshape(n_branch, -1, width).astype(jnp.float32), axis=0
    )
    mean_block = (summed / n_branch).astype(jnp.bfloat16)
    mean_block, all_grads = lax.optimization_barrier((mean_block, all_grads))
    attended = jnp.dot(
        context,
        lax.all_gather(mean_block, "dp", axis=0, tiled=True),
        preferred_element_type=jnp.float32,
    )
    hidden = (hidden_in.astype(jnp.float32) + attended).astype(jnp.bfloat16)
    doubled = jnp.repeat(hidden, 2, axis=0)
    send_rows = (
        jnp.dot(placing, doubled, preferred_element_type=jnp.float32)
        .astype(jnp.bfloat16)
        .reshape(n_branch, capacity, width)
    )
    weight_gate = w_gate[0]
    weight_up = w_up[0]
    weight_down = w_down[0]
    got_rows = lax.all_to_all(send_rows, "branch", split_axis=0, concat_axis=2, tiled=True)
    all_rows = lax.all_gather(got_rows, "dp", axis=1, tiled=True)
    rows_two = all_rows[0]
    grads_two = all_grads[0]
    gate_pre = jnp.dot(rows_two, weight_gate, preferred_element_type=jnp.float32)
    up_pre = jnp.dot(rows_two, weight_up, preferred_element_type=jnp.float32)
    d_act = jnp.einsum("rd,fd->rf", grads_two, weight_down, preferred_element_type=jnp.float32)
    act, d_gate, d_up = swiglu_parts(gate_pre, up_pre, d_act)
    grad_gate = jnp.einsum("rd,rf->df", rows_two, d_gate, preferred_element_type=jnp.float32)
    grad_up = jnp.einsum("rd,rf->df", rows_two, d_up, preferred_element_type=jnp.float32)
    grad_down = jnp.einsum("rf,rd->fd", act, grads_two, preferred_element_type=jnp.float32)
    output_term = jnp.dot(act, weight_down, preferred_element_type=jnp.float32)
    input_term = jnp.einsum(
        "rf,df->rd", d_gate, weight_gate, preferred_element_type=jnp.float32
    ) + jnp.einsum("rf,df->rd", d_up, weight_up, preferred_element_type=jnp.float32)
    out_part = lax.psum_scatter(
        output_term.astype(jnp.bfloat16), "dp", scatter_dimension=0, tiled=True
    )
    in_part = lax.psum_scatter(
        input_term.astype(jnp.bfloat16), "dp", scatter_dimension=0, tiled=True
    )
    packed = jnp.stack(
        [
            out_part.reshape(capacity, n_branch, width),
            in_part.reshape(capacity, n_branch, width),
        ],
        axis=2,
    ).transpose(1, 0, 2, 3)
    returned = lax.all_to_all(packed, "branch", split_axis=0, concat_axis=0, tiled=True)
    picked = jnp.einsum(
        "sr,sc->rc",
        placing,
        returned.reshape(n_branch * capacity, 2 * width),
        preferred_element_type=jnp.float32,
    )
    picked = picked.reshape(rows_tok, 2, 2, width)
    mixed = (
        hidden.astype(jnp.float32) + jnp.sum(share[:, :, None] * picked[:, :, 0], axis=1)
    ).astype(jnp.bfloat16)
    input_grad = (cotangent.astype(jnp.float32) + jnp.sum(picked[:, :, 1], axis=1)).astype(
        jnp.bfloat16
    )
    return (
        mixed,
        input_grad,
        grad_gate.astype(jnp.bfloat16)[None],
        grad_up.astype(jnp.bfloat16)[None],
        grad_down.astype(jnp.bfloat16)[None],
    )


def solution(mesh):
    return jax.shard_map(
        shards,
        mesh=mesh,
        in_specs=(
            P("dp", "branch"),
            P("dp", None),
            P("branch", "dp", None),
            P("dp", None),
            P("dp", None),
            P("branch", None, "dp"),
            P("branch", None, "dp"),
            P("branch", "dp", None),
            P("dp", "branch"),
        ),
        out_specs=(
            P("dp", "branch"),
            P("dp", "branch"),
            P("branch", None, "dp"),
            P("branch", None, "dp"),
            P("branch", "dp", None),
        ),
        check_vma=False,
    )
```

```python
import jax
import jax.numpy as jnp
from jax import lax
from jax.sharding import PartitionSpec as P


def swiglu_parts(gate_pre, up_pre, d_act):
    sigma = jax.nn.sigmoid(gate_pre)
    silu = gate_pre * sigma
    act = (silu * up_pre).astype(jnp.bfloat16)
    d_gate = (d_act * up_pre * sigma * (1.0 + gate_pre * (1.0 - sigma))).astype(jnp.bfloat16)
    d_up = (d_act * silu).astype(jnp.bfloat16)
    return (act, d_gate, d_up)


def shards(hidden_in, context, branch_wo, expert_ids, gate_num, w_gate, w_up, w_down, cotangent):
    n_branch = lax.axis_size("branch")
    rows_tok, width = hidden_in.shape
    model_width = context.shape[1]
    capacity = 3 * rows_tok // n_branch
    flat_ids = expert_ids.reshape(-1)
    labels = jnp.arange(n_branch, dtype=jnp.int32)
    onehot = (flat_ids[:, None] == labels[None, :]).astype(jnp.int32)
    before = jnp.cumsum(onehot, axis=0) - onehot
    slot = flat_ids * capacity + jnp.sum(before * onehot, axis=1)
    placing = (jnp.arange(n_branch * capacity, dtype=jnp.int32)[:, None] == slot[None, :]).astype(
        jnp.bfloat16
    )
    share = gate_num.astype(jnp.float32)
    share = share / jnp.sum(share, axis=1, keepdims=True)
    weighted = (
        share.reshape(-1)[:, None] * jnp.repeat(cotangent.astype(jnp.float32), 2, axis=0)
    ).astype(jnp.bfloat16)
    send_grads = (
        jnp.dot(placing, weighted, preferred_element_type=jnp.float32)
        .astype(jnp.bfloat16)
        .reshape(n_branch, capacity, width)
    )
    got_grads = lax.all_to_all(send_grads, "branch", split_axis=0, concat_axis=2, tiled=True)
    all_grads = lax.all_gather(got_grads, "dp", axis=1, tiled=True)
    got_grads, wo_local = lax.optimization_barrier((got_grads, branch_wo[0]))
    pieces = lax.all_to_all(wo_local, "branch", split_axis=1, concat_axis=0, tiled=True)
    summed = jnp.sum(
        pieces.reshape(n_branch, -1, width).astype(jnp.float32), axis=0
    )
    mean_block = (summed / n_branch).astype(jnp.bfloat16)
    mean_block, all_grads = lax.optimization_barrier((mean_block, all_grads))
    attended = jnp.dot(
        context,
        lax.all_gather(mean_block, "dp", axis=0, tiled=True),
        preferred_element_type=jnp.float32,
    )
    hidden = (hidden_in.astype(jnp.float32) + attended).astype(jnp.bfloat16)
    doubled = jnp.repeat(hidden, 2, axis=0)
    send_rows = (
        jnp.dot(placing, doubled, preferred_element_type=jnp.float32)
        .astype(jnp.bfloat16)
        .reshape(n_branch, capacity, width)
    )
    weight_gate = w_gate[0]
    weight_up = w_up[0]
    weight_down = w_down[0]
    got_rows = lax.all_to_all(send_rows, "branch", split_axis=0, concat_axis=2, tiled=True)
    all_rows = lax.all_gather(got_rows, "dp", axis=1, tiled=True)
    rows_two = all_rows[0]
    grads_two = all_grads[0]
    gate_pre = jnp.dot(rows_two, weight_gate, preferred_element_type=jnp.float32)
    up_pre = jnp.dot(rows_two, weight_up, preferred_element_type=jnp.float32)
    d_act = jnp.einsum("rd,fd->rf", grads_two, weight_down, preferred_element_type=jnp.float32)
    act, d_gate, d_up = swiglu_parts(gate_pre, up_pre, d_act)
    grad_gate = jnp.einsum("rd,rf->df", rows_two, d_gate, preferred_element_type=jnp.float32)
    grad_up = jnp.einsum("rd,rf->df", rows_two, d_up, preferred_element_type=jnp.float32)
    grad_down = jnp.einsum("rf,rd->fd", act, grads_two, preferred_element_type=jnp.float32)
    output_term = jnp.dot(act, weight_down, preferred_element_type=jnp.float32)
    input_term = jnp.einsum(
        "rf,df->rd", d_gate, weight_gate, preferred_element_type=jnp.float32
    ) + jnp.einsum("rf,df->rd", d_up, weight_up, preferred_element_type=jnp.float32)
    out_part = lax.psum_scatter(
        output_term.astype(jnp.bfloat16), "dp", scatter_dimension=0, tiled=True
    )
    grad_gate = grad_gate.astype(jnp.bfloat16)[None]
    grad_up = grad_up.astype(jnp.bfloat16)[None]
    grad_down = grad_down.astype(jnp.bfloat16)[None]
    input_bf, grad_gate, grad_up, grad_down = lax.optimization_barrier(
        (input_term.astype(jnp.bfloat16), grad_gate, grad_up, grad_down)
    )
    in_part = lax.psum_scatter(input_bf, "dp", scatter_dimension=0, tiled=True)
    packed = jnp.stack(
        [
            out_part.reshape(capacity, n_branch, width),
            in_part.reshape(capacity, n_branch, width),
        ],
        axis=2,
    ).transpose(1, 0, 2, 3)
    returned = lax.all_to_all(packed, "branch", split_axis=0, concat_axis=0, tiled=True)
    picked = jnp.einsum(
        "sr,sc->rc",
        placing,
        returned.reshape(n_branch * capacity, 2 * width),
        preferred_element_type=jnp.float32,
    )
    picked = picked.reshape(rows_tok, 2, 2, width)
    mixed = (
        hidden.astype(jnp.float32) + jnp.sum(share[:, :, None] * picked[:, :, 0], axis=1)
    ).astype(jnp.bfloat16)
    input_grad = (cotangent.astype(jnp.float32) + jnp.sum(picked[:, :, 1], axis=1)).astype(
        jnp.bfloat16
    )
    return (
        mixed,
        input_grad,
        grad_gate,
        grad_up,
        grad_down,
    )


def solution(mesh):
    return jax.shard_map(
        shards,
        mesh=mesh,
        in_specs=(
            P("dp", "branch"),
            P("dp", None),
            P("branch", "dp", None),
            P("dp", None),
            P("dp", None),
            P("branch", None, "dp"),
            P("branch", None, "dp"),
            P("branch", "dp", None),
            P("dp", "branch"),
        ),
        out_specs=(
            P("dp", "branch"),
            P("dp", "branch"),
            P("branch", None, "dp"),
            P("branch", None, "dp"),
            P("branch", "dp", None),
        ),
        check_vma=False,
    )
```

```python
import jax
import jax.numpy as jnp
from jax import lax
from jax.sharding import PartitionSpec as P


def swiglu_parts(gate_pre, up_pre, d_act):
    sigma = jax.nn.sigmoid(gate_pre)
    silu = gate_pre * sigma
    act = (silu * up_pre).astype(jnp.bfloat16)
    d_gate = (d_act * up_pre * sigma * (1.0 + gate_pre * (1.0 - sigma))).astype(jnp.bfloat16)
    d_up = (d_act * silu).astype(jnp.bfloat16)
    return (act, d_gate, d_up)


def shards(hidden_in, context, branch_wo, expert_ids, gate_num, w_gate, w_up, w_down, cotangent):
    n_branch = lax.axis_size("branch")
    rows_tok, width = hidden_in.shape
    model_width = context.shape[1]
    capacity = 3 * rows_tok // n_branch
    flat_ids = expert_ids.reshape(-1)
    labels = jnp.arange(n_branch, dtype=jnp.int32)
    onehot = (flat_ids[:, None] == labels[None, :]).astype(jnp.int32)
    before = jnp.cumsum(onehot, axis=0) - onehot
    slot = flat_ids * capacity + jnp.sum(before * onehot, axis=1)
    placing = (jnp.arange(n_branch * capacity, dtype=jnp.int32)[:, None] == slot[None, :]).astype(
        jnp.bfloat16
    )
    share = gate_num.astype(jnp.float32)
    share = share / jnp.sum(share, axis=1, keepdims=True)
    weighted = (
        share.reshape(-1)[:, None] * jnp.repeat(cotangent.astype(jnp.float32), 2, axis=0)
    ).astype(jnp.bfloat16)
    send_grads = (
        jnp.dot(placing, weighted, preferred_element_type=jnp.float32)
        .astype(jnp.bfloat16)
        .reshape(n_branch, capacity, width)
    )
    pieces = lax.all_to_all(branch_wo[0], "branch", split_axis=1, concat_axis=0, tiled=True)
    pieces, send_grads = lax.optimization_barrier((pieces, send_grads))
    summed = jnp.sum(
        pieces.reshape(n_branch, -1, width).astype(jnp.float32), axis=0
    )
    mean_block = (summed / n_branch).astype(jnp.bfloat16)
    wo_full = lax.all_gather(mean_block, "dp", axis=0, tiled=True)
    got_grads = lax.all_to_all(send_grads, "branch", split_axis=0, concat_axis=2, tiled=True)
    got_grads, wo_full = lax.optimization_barrier((got_grads, wo_full))
    all_grads = lax.all_gather(got_grads, "dp", axis=1, tiled=True)
    attended = jnp.dot(context, wo_full, preferred_element_type=jnp.float32)
    hidden = (hidden_in.astype(jnp.float32) + attended).astype(jnp.bfloat16)
    doubled = jnp.repeat(hidden, 2, axis=0)
    send_rows = (
        jnp.dot(placing, doubled, preferred_element_type=jnp.float32)
        .astype(jnp.bfloat16)
        .reshape(n_branch, capacity, width)
    )
    weight_gate = w_gate[0]
    weight_up = w_up[0]
    weight_down = w_down[0]
    got_rows = lax.all_to_all(send_rows, "branch", split_axis=0, concat_axis=2, tiled=True)
    got_rows, all_grads = lax.optimization_barrier((got_rows, all_grads))
    all_rows = lax.all_gather(got_rows, "dp", axis=1, tiled=True)
    rows_two = all_rows[0]
    grads_two = all_grads[0]
    gate_pre = jnp.dot(rows_two, weight_gate, preferred_element_type=jnp.float32)
    up_pre = jnp.dot(rows_two, weight_up, preferred_element_type=jnp.float32)
    d_act = jnp.einsum("rd,fd->rf", grads_two, weight_down, preferred_element_type=jnp.float32)
    act, d_gate, d_up = swiglu_parts(gate_pre, up_pre, d_act)
    grad_gate = jnp.einsum("rd,rf->df", rows_two, d_gate, preferred_element_type=jnp.float32)
    grad_up = jnp.einsum("rd,rf->df", rows_two, d_up, preferred_element_type=jnp.float32)
    grad_down = jnp.einsum("rf,rd->fd", act, grads_two, preferred_element_type=jnp.float32)
    output_term = jnp.dot(act, weight_down, preferred_element_type=jnp.float32)
    input_term = jnp.einsum(
        "rf,df->rd", d_gate, weight_gate, preferred_element_type=jnp.float32
    ) + jnp.einsum("rf,df->rd", d_up, weight_up, preferred_element_type=jnp.float32)
    out_part = lax.psum_scatter(
        output_term.astype(jnp.bfloat16), "dp", scatter_dimension=0, tiled=True
    )
    in_part = lax.psum_scatter(
        input_term.astype(jnp.bfloat16), "dp", scatter_dimension=0, tiled=True
    )
    packed = jnp.stack(
        [
            out_part.reshape(capacity, n_branch, width),
            in_part.reshape(capacity, n_branch, width),
        ],
        axis=2,
    ).transpose(1, 0, 2, 3)
    returned = lax.all_to_all(packed, "branch", split_axis=0, concat_axis=0, tiled=True)
    picked = jnp.einsum(
        "sr,sc->rc",
        placing,
        returned.reshape(n_branch * capacity, 2 * width),
        preferred_element_type=jnp.float32,
    )
    picked = picked.reshape(rows_tok, 2, 2, width)
    mixed = (
        hidden.astype(jnp.float32) + jnp.sum(share[:, :, None] * picked[:, :, 0], axis=1)
    ).astype(jnp.bfloat16)
    input_grad = (cotangent.astype(jnp.float32) + jnp.sum(picked[:, :, 1], axis=1)).astype(
        jnp.bfloat16
    )
    return (
        mixed,
        input_grad,
        grad_gate.astype(jnp.bfloat16)[None],
        grad_up.astype(jnp.bfloat16)[None],
        grad_down.astype(jnp.bfloat16)[None],
    )


def solution(mesh):
    return jax.shard_map(
        shards,
        mesh=mesh,
        in_specs=(
            P("dp", "branch"),
            P("dp", None),
            P("branch", "dp", None),
            P("dp", None),
            P("dp", None),
            P("branch", None, "dp"),
            P("branch", None, "dp"),
            P("branch", "dp", None),
            P("dp", "branch"),
        ),
        out_specs=(
            P("dp", "branch"),
            P("dp", "branch"),
            P("branch", None, "dp"),
            P("branch", None, "dp"),
            P("branch", "dp", None),
        ),
        check_vma=False,
    )
```

```python
import jax
import jax.numpy as jnp
from jax import lax
from jax.sharding import PartitionSpec as P


def swiglu_parts(gate_pre, up_pre, d_act):
    sigma = jax.nn.sigmoid(gate_pre)
    silu = gate_pre * sigma
    act = (silu * up_pre).astype(jnp.bfloat16)
    d_gate = (d_act * up_pre * sigma * (1.0 + gate_pre * (1.0 - sigma))).astype(jnp.bfloat16)
    d_up = (d_act * silu).astype(jnp.bfloat16)
    return (act, d_gate, d_up)


def shards(hidden_in, context, branch_wo, expert_ids, gate_num, w_gate, w_up, w_down, cotangent):
    n_branch = lax.axis_size("branch")
    rows_tok, width = hidden_in.shape
    model_width = context.shape[1]
    capacity = 3 * rows_tok // n_branch
    flat_ids = expert_ids.reshape(-1)
    labels = jnp.arange(n_branch, dtype=jnp.int32)
    onehot = (flat_ids[:, None] == labels[None, :]).astype(jnp.int32)
    before = jnp.cumsum(onehot, axis=0) - onehot
    slot = flat_ids * capacity + jnp.sum(before * onehot, axis=1)
    placing = (jnp.arange(n_branch * capacity, dtype=jnp.int32)[:, None] == slot[None, :]).astype(
        jnp.bfloat16
    )
    share = gate_num.astype(jnp.float32)
    share = share / jnp.sum(share, axis=1, keepdims=True)
    weighted = (
        share.reshape(-1)[:, None] * jnp.repeat(cotangent.astype(jnp.float32), 2, axis=0)
    ).astype(jnp.bfloat16)
    send_grads = (
        jnp.dot(placing, weighted, preferred_element_type=jnp.float32)
        .astype(jnp.bfloat16)
        .reshape(n_branch, capacity, width)
    )
    pieces = lax.all_to_all(branch_wo[0], "branch", split_axis=1, concat_axis=1, tiled=True)
    pieces, send_grads = lax.optimization_barrier((pieces, send_grads))
    summed = jnp.sum(
        pieces.reshape(-1, n_branch, width).astype(jnp.float32), axis=1
    )
    mean_block = (summed / n_branch).astype(jnp.bfloat16)
    wo_full = lax.all_gather(mean_block, "dp", axis=0, tiled=True)
    got_grads = lax.all_to_all(send_grads, "branch", split_axis=0, concat_axis=2, tiled=True)
    got_grads, wo_full = lax.optimization_barrier((got_grads, wo_full))
    all_grads = lax.all_gather(got_grads, "dp", axis=1, tiled=True)
    attended = jnp.dot(context, wo_full, preferred_element_type=jnp.float32)
    hidden = (hidden_in.astype(jnp.float32) + attended).astype(jnp.bfloat16)
    doubled = jnp.repeat(hidden, 2, axis=0)
    send_rows = (
        jnp.dot(placing, doubled, preferred_element_type=jnp.float32)
        .astype(jnp.bfloat16)
        .reshape(n_branch, capacity, width)
    )
    weight_gate = w_gate[0]
    weight_up = w_up[0]
    weight_down = w_down[0]
    got_rows = lax.all_to_all(send_rows, "branch", split_axis=0, concat_axis=2, tiled=True)
    got_rows, all_grads = lax.optimization_barrier((got_rows, all_grads))
    all_rows = lax.all_gather(got_rows, "dp", axis=1, tiled=True)
    rows_two = all_rows[0]
    grads_two = all_grads[0]
    gate_pre = jnp.dot(rows_two, weight_gate, preferred_element_type=jnp.float32)
    up_pre = jnp.dot(rows_two, weight_up, preferred_element_type=jnp.float32)
    d_act = jnp.einsum("rd,fd->rf", grads_two, weight_down, preferred_element_type=jnp.float32)
    act, d_gate, d_up = swiglu_parts(gate_pre, up_pre, d_act)
    grad_gate = jnp.einsum("rd,rf->df", rows_two, d_gate, preferred_element_type=jnp.float32)
    grad_up = jnp.einsum("rd,rf->df", rows_two, d_up, preferred_element_type=jnp.float32)
    grad_down = jnp.einsum("rf,rd->fd", act, grads_two, preferred_element_type=jnp.float32)
    output_term = jnp.dot(act, weight_down, preferred_element_type=jnp.float32)
    input_term = jnp.einsum(
        "rf,df->rd", d_gate, weight_gate, preferred_element_type=jnp.float32
    ) + jnp.einsum("rf,df->rd", d_up, weight_up, preferred_element_type=jnp.float32)
    out_part = lax.psum_scatter(
        output_term.astype(jnp.bfloat16), "dp", scatter_dimension=0, tiled=True
    )
    in_part = lax.psum_scatter(
        input_term.astype(jnp.bfloat16), "dp", scatter_dimension=0, tiled=True
    )
    packed = jnp.stack(
        [
            out_part.reshape(capacity, n_branch, width),
            in_part.reshape(capacity, n_branch, width),
        ],
        axis=2,
    ).transpose(1, 0, 2, 3)
    returned = lax.all_to_all(packed, "branch", split_axis=0, concat_axis=0, tiled=True)
    picked = jnp.einsum(
        "sr,sc->rc",
        placing,
        returned.reshape(n_branch * capacity, 2 * width),
        preferred_element_type=jnp.float32,
    )
    picked = picked.reshape(rows_tok, 2, 2, width)
    mixed = (
        hidden.astype(jnp.float32) + jnp.sum(share[:, :, None] * picked[:, :, 0], axis=1)
    ).astype(jnp.bfloat16)
    input_grad = (cotangent.astype(jnp.float32) + jnp.sum(picked[:, :, 1], axis=1)).astype(
        jnp.bfloat16
    )
    return (
        mixed,
        input_grad,
        grad_gate.astype(jnp.bfloat16)[None],
        grad_up.astype(jnp.bfloat16)[None],
        grad_down.astype(jnp.bfloat16)[None],
    )


def solution(mesh):
    return jax.shard_map(
        shards,
        mesh=mesh,
        in_specs=(
            P("dp", "branch"),
            P("dp", None),
            P("branch", "dp", None),
            P("dp", None),
            P("dp", None),
            P("branch", None, "dp"),
            P("branch", None, "dp"),
            P("branch", "dp", None),
            P("dp", "branch"),
        ),
        out_specs=(
            P("dp", "branch"),
            P("dp", "branch"),
            P("branch", None, "dp"),
            P("branch", None, "dp"),
            P("branch", "dp", None),
        ),
        check_vma=False,
    )
```
